32 devices in a mesh: replica: 2 (over y), shard: 16 (over z, x, core).
Axes of the slice: x: 2, y: 2, z: 4, core: 2. Of those that a mesh axis runs over, the one named last changes fastest.
Arguments:
- hidden_in: float32 [8192, 1024], P(('replica', 'shard')), may hold values from -6 to 6
- segment_ids: int32 [8192], P(('replica', 'shard')), may hold values from 0 to 8191, as said below
- positions: int32 [8192], P(('replica', 'shard')), may hold values from 0 to 1023, as said below
- ln_gain: bfloat16 [1024], P('shard'), may hold values from 0.5 to 1.5
- ln_bias: bfloat16 [1024], P('shard'), may hold values from -3 to 3
- w_qkv: bfloat16 [1024, 3072], P('shard'), as said below
- b_query: bfloat16 [1024], P('shard'), may hold values from -3 to 3
- b_key: bfloat16 [512], P('shard'), may hold values from -3 to 3
- b_value: bfloat16 [1024], P('shard'), may hold values from -3 to 3
- w_dense: bfloat16 [1024, 1024], P('shard'), may hold values from -0.75 to 0.75
- b_dense: bfloat16 [1024], P('shard'), may hold values from -3 to 3
- w_fc1: bfloat16 [1024, 4096], P('shard'), may hold values from -0.1875 to 0.1875
- b_fc1: bfloat16 [4096], P('shard'), may hold values from -3 to 3
- w_fc2: bfloat16 [4096, 1024], P('shard'), may hold values from -0.09375 to 0.09375
- b_fc2: bfloat16 [1024], P('shard'), may hold values from -3 to 3
- cotangent: float32 [8192, 1024], P(('replica', 'shard')), may hold values from -6 to 6
Outputs:
- block_out: float32 [8192, 1024], P(('replica', 'shard'))
- grad_input: float32 [8192, 1024], P(('replica', 'shard'))
- grad_ln_gain: float32 [1024], P('shard')
- grad_ln_bias: float32 [1024], P('shard')
- grad_w_qkv: float32 [1024, 3072], P('shard')
- grad_b_query: float32 [1024], P('shard')
- grad_b_key: float32 [512], P('shard')
- grad_b_value: float32 [1024], P('shard')
- grad_w_dense: float32 [1024, 1024], P('shard')
- grad_b_dense: float32 [1024], P('shard')
- grad_w_fc1: float32 [1024, 4096], P('shard')
- grad_b_fc1: float32 [4096], P('shard')
- grad_w_fc2: float32 [4096, 1024], P('shard')
- grad_b_fc2: float32 [1024], P('shard')
The draws below stay inside these ranges and needn't reach their ends.
Inputs may be any that keep to these rules, and one draw needn't show every extreme that they name: `segment_ids`: within each aligned block of 256 tokens (one sequence) the ids never fall, lie from the block's first token index to its last, and no id appears in two blocks. Within a segment the positions rise by one from token to token; a segment that does not open its block of 256 tokens starts at 0. `w_qkv`: entries scaled by the root of the fan-in 1024.
All inputs are finite; a program needn't handle non-finite values.
Results may differ from the reference program's by a relative error of at most 0.012.
Values may be sent and summed in bfloat16 or wider, within the bound.
No kernel may reach another device: no remote copies, remote signals or barrier semaphores. Data moves between devices by JAX's collectives and lax.ppermute only.
A program may use at most 320 MiB of HBM per device.

```python
import math
import jax
import jax.numpy as jnp
from jax import lax

MODEL_WIDTH = 1024
ATTENTION_HEADS = 16
HEAD_DIM = 64
ROTARY_FEATURES = 32
FF = 4096
LEN = 256
TOKENS = 8192


def segment_layout(key):
    base = jax.random.fold_in(key, 5)
    first_key, second_key = jax.random.split(base)
    rows = TOKENS // LEN
    rolls = jax.random.randint(first_key, (rows, LEN), 0, max(LEN // 8, 4))
    column = jnp.broadcast_to(jnp.arange(LEN, dtype=jnp.int32)[None, :], (rows, LEN))
    row_index = jnp.broadcast_to(jnp.arange(rows, dtype=jnp.int32)[:, None], (rows, LEN))
    last_row = row_index == rows - 1
    starts_here = (rolls == 0) & jnp.logical_not(last_row) | (column == 0)
    local = jnp.cumsum(starts_here.astype(jnp.int32), axis=1) - 1
    begin = lax.cummax(jnp.where(starts_here, column, 0), axis=1)
    offset = jax.random.randint(second_key, (rows, 1), 0, 1024 - LEN + 1)
    offset = jnp.where(jnp.arange(rows, dtype=jnp.int32)[:, None] == 0, 0, offset)
    offset = jnp.where(jnp.arange(rows, dtype=jnp.int32)[:, None] == rows - 1, 1024 - LEN, offset)
    pos = column - begin + jnp.where(local == 0, offset, 0)
    shift = jnp.where(last_row, LEN - 1, 0)
    seg = local + shift + row_index * LEN
    return (seg.reshape(TOKENS).astype(jnp.int32), pos.reshape(TOKENS).astype(jnp.int32))


def draw_segment_ids(key, part):
    return segment_layout(key)[0]


def draw_positions(key, part):
    return segment_layout(key)[1]


def draw_w_qkv(key, part):
    first_key = jax.random.fold_in(jax.random.fold_in(key, 11), 0)
    base = jax.random.normal(first_key, (MODEL_WIDTH, 3 * MODEL_WIDTH), jnp.float32) * MODEL_WIDTH ** (-0.5)
    return base.astype(jnp.bfloat16)


def level_of(key, shape, shards, low, largest):
    gain = 1.0
    for dim, shards_of in shards:
        draws = jax.random.uniform(jax.random.fold_in(jax.random.fold_in(key, 6), dim), (shards_of,), jnp.float32, low / len(shards), largest / len(shards))
        gain = gain * jnp.repeat(jnp.exp(draws), shape[dim] // shards_of).reshape((-1,) + (1,) * (len(shape) - 1 - dim))
    return gain


def gaussian(rng, shape, width, reach, cuts=(), held_as=jnp.bfloat16):
    values = jax.random.normal(rng, shape, jnp.float32) * width
    if len(cuts) > 0:
        values = level_of(rng, shape, cuts, -0.22, 0.18) * values
    return jnp.clip(values, min=-reach, max=reach).astype(held_as)


def setup_inputs(seed: int = 0) -> dict:
    key_of = jax.random.split(jax.random.key(seed), 17)
    return {
        "hidden_in": gaussian(key_of[0], (TOKENS, MODEL_WIDTH), 1.0, 6.0, ((0, 32),), jnp.float32),
        "segment_ids": draw_segment_ids(jax.random.fold_in(key_of[16], 71), 0),
        "positions": draw_positions(jax.random.fold_in(key_of[16], 71), 0),
        "ln_gain": jnp.clip(1.0 + 0.1 * jax.random.normal(key_of[3], (MODEL_WIDTH,), jnp.float32), 0.5, 1.5).astype(jnp.bfloat16),
        "ln_bias": gaussian(key_of[4], (MODEL_WIDTH,), 0.5, 3.0, ((0, 16),)),
        "w_qkv": draw_w_qkv(jax.random.fold_in(key_of[16], 71), 0),
        "b_query": gaussian(key_of[6], (MODEL_WIDTH,), 0.5, 3.0, ((0, 16),)),
        "b_key": gaussian(key_of[7], (ATTENTION_HEADS * ROTARY_FEATURES,), 0.5, 3.0, ((0, 16),)),
        "b_value": gaussian(key_of[8], (MODEL_WIDTH,), 0.5, 3.0, ((0, 16),)),
        "w_dense": gaussian(key_of[9], (MODEL_WIDTH, MODEL_WIDTH), (MODEL_WIDTH // 16) ** -0.5, 0.75, ((0, 16),)),
        "b_dense": gaussian(key_of[10], (MODEL_WIDTH,), 0.5, 3.0, ((0, 16),)),
        "w_fc1": gaussian(key_of[11], (MODEL_WIDTH, FF), MODEL_WIDTH ** -0.5, 0.1875, ((0, 16),)),
        "b_fc1": gaussian(key_of[12], (FF,), 0.5, 3.0, ((0, 16),)),
        "w_fc2": gaussian(key_of[13], (FF, MODEL_WIDTH), FF ** -0.5, 0.09375, ((0, 16),)),
        "b_fc2": gaussian(key_of[14], (MODEL_WIDTH,), 0.5, 3.0, ((0, 16),)),
        "cotangent": gaussian(key_of[15], (TOKENS, MODEL_WIDTH), 1.0, 6.0, ((0, 32),), jnp.float32),
    }


def product(form, left, right):
    return jnp.einsum(form, left.astype(jnp.float32), right.astype(jnp.float32))

def layer_normalize(hidden_state):
    center = hidden_state - lax.optimization_barrier(jnp.mean(hidden_state, axis=-1, keepdims=True))
    variance = lax.optimization_barrier(jnp.mean(center * center, axis=-1, keepdims=True))
    inverse_deviation = lax.rsqrt(variance + 1e-05)
    return (center * inverse_deviation, inverse_deviation)

def rotary_tables(positions):
    half = ROTARY_FEATURES // 2
    freqs = 10000.0 ** (-(jnp.arange(half, dtype=jnp.float32) * 2.0 / ROTARY_FEATURES))
    angles = positions.astype(jnp.float32)[:, None] * freqs[None, :]
    return (jnp.cos(angles), jnp.sin(angles))

def rotate(heads, cosine_table, sine_table):
    half = ROTARY_FEATURES // 2
    first = heads[..., :half]
    second = heads[..., half:ROTARY_FEATURES]
    cosine = cosine_table[:, None, :]
    sine = sine_table[:, None, :]
    return jnp.concatenate([first * cosine - second * sine, second * cosine + first * sine, heads[..., ROTARY_FEATURES:]], axis=-1)

def unrotate(heads, cosine_table, sine_table):
    half = ROTARY_FEATURES // 2
    first = heads[..., :half]
    second = heads[..., half:ROTARY_FEATURES]
    cosine = cosine_table[:, None, :]
    sine = sine_table[:, None, :]
    return jnp.concatenate([first * cosine + second * sine, second * cosine - first * sine, heads[..., ROTARY_FEATURES:]], axis=-1)

def gelu_value(up_projection):
    inner = math.sqrt(2.0 / math.pi) * (up_projection + 0.044715 * up_projection * up_projection * up_projection)
    return 0.5 * up_projection * (1.0 + jnp.tanh(inner))

def gelu_slope(up_projection):
    coeff = math.sqrt(2.0 / math.pi)
    tangent = jnp.tanh(coeff * (up_projection + 0.044715 * up_projection * up_projection * up_projection))
    return 0.5 * (1.0 + tangent) + 0.5 * up_projection * (1.0 - tangent * tangent) * coeff * (1.0 + 3.0 * 0.044715 * up_projection * up_projection)

def segment_mask(segment_ids, nseq):
    seg = segment_ids.reshape(nseq, LEN)
    index = jnp.arange(LEN, dtype=jnp.int32)
    causal = index[:, None] >= index[None, :]
    same = seg[:, :, None] == seg[:, None, :]
    return (same & causal[None, :, :])[:, None, :, :]

def attention_scores(query_heads, key_heads, document_mask):
    scores = product('sqhd,skhd->shqk', query_heads, key_heads) * HEAD_DIM ** (-0.5)
    return jnp.where(document_mask, scores, -1e+30)

def forward(hidden_state, segment_ids, positions, params):
    norm_gain, norm_shift, w_qkv, b_query, b_key, b_value, w_dense, b_dense, w_fc1, b_fc1, w_fc2, b_fc2 = params
    tokens = hidden_state.shape[0]
    nseq = tokens // LEN
    centered_input, inverse_deviation = layer_normalize(hidden_state)
    normed_input = (centered_input * norm_gain.astype(jnp.float32) + norm_shift.astype(jnp.float32)).astype(jnp.bfloat16)
    qkv = jnp.dot(normed_input, w_qkv, preferred_element_type=jnp.float32)
    key_bias = jnp.concatenate([b_key.astype(jnp.float32).reshape(ATTENTION_HEADS, ROTARY_FEATURES), jnp.zeros((ATTENTION_HEADS, HEAD_DIM - ROTARY_FEATURES), jnp.float32)], axis=1)
    query = qkv[:, :MODEL_WIDTH].reshape(tokens, ATTENTION_HEADS, HEAD_DIM) + b_query.astype(jnp.float32).reshape(ATTENTION_HEADS, HEAD_DIM)
    keys = qkv[:, MODEL_WIDTH:2 * MODEL_WIDTH].reshape(tokens, ATTENTION_HEADS, HEAD_DIM) + key_bias
    values = qkv[:, 2 * MODEL_WIDTH:] + b_value.astype(jnp.float32)
    cosine_table, sine_table = rotary_tables(positions)
    query_heads = rotate(query, cosine_table, sine_table).astype(jnp.bfloat16).reshape(nseq, LEN, ATTENTION_HEADS, HEAD_DIM)
    key_heads = rotate(keys, cosine_table, sine_table).astype(jnp.bfloat16).reshape(nseq, LEN, ATTENTION_HEADS, HEAD_DIM)
    value_heads = values.astype(jnp.bfloat16).reshape(nseq, LEN, ATTENTION_HEADS, HEAD_DIM)
    document_mask = segment_mask(segment_ids, nseq)
    scores = attention_scores(query_heads, key_heads, document_mask)
    top = lax.optimization_barrier(jnp.max(scores, axis=-1, keepdims=True))
    expo = jnp.exp(scores - top)
    total = lax.optimization_barrier(jnp.sum(expo, axis=-1, keepdims=True))
    log_sum_exp = top + jnp.log(total)
    probs = (expo / total).astype(jnp.bfloat16)
    attended_values = product('shqk,skhd->sqhd', probs, value_heads).reshape(tokens, MODEL_WIDTH).astype(jnp.bfloat16)
    attn_out = jnp.dot(attended_values, w_dense, preferred_element_type=jnp.float32) + b_dense.astype(jnp.float32)
    up_projection = jnp.dot(normed_input, w_fc1, preferred_element_type=jnp.float32) + b_fc1.astype(jnp.float32)
    activation = gelu_value(up_projection).astype(jnp.bfloat16)
    mlp_out = jnp.dot(activation, w_fc2, preferred_element_type=jnp.float32) + b_fc2.astype(jnp.float32)
    saved_residuals = (centered_input, inverse_deviation, normed_input, query_heads, key_heads, value_heads, log_sum_exp, attended_values, up_projection, activation, cosine_table, sine_table, document_mask)
    return (hidden_state + attn_out + mlp_out, saved_residuals)

def backward(saved_residuals, upstream_gradient, norm_gain, w_qkv, w_dense, w_fc1, w_fc2):
    centered_input, inverse_deviation, normed_input, query_heads, key_heads, value_heads, log_sum_exp, attended_values, up_projection, activation, cosine_table, sine_table, document_mask = saved_residuals
    tokens = upstream_gradient.shape[0]
    output_cotangent = upstream_gradient.astype(jnp.bfloat16)
    d_attended = jnp.dot(output_cotangent, w_dense.T, preferred_element_type=jnp.float32).astype(jnp.bfloat16).reshape(query_heads.shape)
    d_act = jnp.dot(output_cotangent, w_fc2.T, preferred_element_type=jnp.float32)
    up_gradient = d_act * gelu_slope(up_projection)
    up_bias_gradient = up_gradient.astype(jnp.bfloat16)
    normed_gradient = jnp.dot(up_bias_gradient, w_fc1.T, preferred_element_type=jnp.float32)
    scores = attention_scores(query_heads, key_heads, document_mask)
    rprobs = jnp.exp(scores - log_sum_exp)
    probs_b = rprobs.astype(jnp.bfloat16)
    value_gradient = product('shqk,sqhd->skhd', probs_b, d_attended)
    d_probs = product('sqhd,skhd->shqk', d_attended, value_heads)
    delta = lax.optimization_barrier(jnp.sum(rprobs * d_probs, axis=-1, keepdims=True))
    d_scores = (rprobs * (d_probs - delta)).astype(jnp.bfloat16)
    scale = HEAD_DIM ** (-0.5)
    query_gradient = product('shqk,skhd->sqhd', d_scores, key_heads) * scale
    key_gradient = product('shqk,sqhd->skhd', d_scores, query_heads) * scale
    query_gradient = unrotate(query_gradient.reshape(tokens, ATTENTION_HEADS, HEAD_DIM), cosine_table, sine_table)
    key_gradient = unrotate(key_gradient.reshape(tokens, ATTENTION_HEADS, HEAD_DIM), cosine_table, sine_table)
    value_gradient = value_gradient.reshape(tokens, MODEL_WIDTH)
    projection_gradient = jnp.concatenate([query_gradient.reshape(tokens, MODEL_WIDTH), key_gradient.reshape(tokens, MODEL_WIDTH), value_gradient], axis=1).astype(jnp.bfloat16)
    normed_gradient = normed_gradient + jnp.dot(projection_gradient, w_qkv.T, preferred_element_type=jnp.float32)
    scaled_scores = normed_gradient * norm_gain.astype(jnp.float32)
    input_gradient = upstream_gradient + inverse_deviation * (scaled_scores - lax.optimization_barrier(jnp.mean(scaled_scores, axis=-1, keepdims=True)) - centered_input * lax.optimization_barrier(jnp.mean(scaled_scores * centered_input, axis=-1, keepdims=True)))
    output_sum = lax.optimization_barrier(jnp.sum(upstream_gradient, axis=0))
    weight_gradients = (lax.optimization_barrier(jnp.sum(normed_gradient * centered_input, axis=0)), lax.optimization_barrier(jnp.sum(normed_gradient, axis=0)), jnp.dot(normed_input.T, projection_gradient, preferred_element_type=jnp.float32), lax.optimization_barrier(jnp.sum(query_gradient, axis=0)).reshape(MODEL_WIDTH), lax.optimization_barrier(jnp.sum(key_gradient[:, :, :ROTARY_FEATURES], axis=0)).reshape(ATTENTION_HEADS * ROTARY_FEATURES), lax.optimization_barrier(jnp.sum(value_gradient, axis=0)), jnp.dot(attended_values.T, output_cotangent, preferred_element_type=jnp.float32), output_sum, jnp.dot(normed_input.T, up_bias_gradient, preferred_element_type=jnp.float32), lax.optimization_barrier(jnp.sum(up_gradient, axis=0)), jnp.dot(activation.T, output_cotangent, preferred_element_type=jnp.float32), output_sum)
    return (input_gradient, weight_gradients)

def reference(hidden_in, segment_ids, positions, ln_gain, ln_bias, w_qkv, b_query, b_key, b_value, w_dense, b_dense, w_fc1, b_fc1, w_fc2, b_fc2, cotangent):
    params = (ln_gain, ln_bias, w_qkv, b_query, b_key, b_value, w_dense, b_dense, w_fc1, b_fc1, w_fc2, b_fc2)
    seqs = TOKENS // LEN
    group = math.gcd(seqs, 16)
    blocks = seqs // group
    rows = group * LEN

    def one_block(accum, items):
        hidden_state, seg, pos, upstream_gradient = items
        out, saved_residuals = forward(hidden_state, seg, pos, params)
        input_gradient, weight_gradients = backward(saved_residuals, upstream_gradient, ln_gain, w_qkv, w_dense, w_fc1, w_fc2)
        return (tuple((a + g for a, g in zip(accum, weight_gradients))), (out, input_gradient))
    zeros = tuple((jnp.zeros(p.shape, jnp.float32) for p in params))
    inputs = (hidden_in.reshape(blocks, rows, MODEL_WIDTH), segment_ids.reshape(blocks, rows), positions.reshape(blocks, rows), cotangent.reshape(blocks, rows, MODEL_WIDTH))
    accum, (outs, grads_in) = lax.scan(one_block, zeros, inputs)
    return (outs.reshape(TOKENS, MODEL_WIDTH), grads_in.reshape(TOKENS, MODEL_WIDTH), accum[0], accum[1], accum[2], accum[3], accum[4], accum[5], accum[6], accum[7], accum[8], accum[9], accum[10], accum[11])
```

```python
import functools
import math

import jax
import jax.numpy as jnp
import numpy as np
from jax import lax
from jax.experimental import pallas as pl
from jax.experimental.pallas import tpu as pltpu
from jax.sharding import Mesh, PartitionSpec as P

HEAD_DIM = 64
ROTARY = 32
LEN = 256
BF = jnp.bfloat16
F32 = jnp.float32
NN = (((1,), (0,)), ((), ()))
NT = (((1,), (1,)), ((), ()))
TN = (((0,), (0,)), ((), ()))


def dot(a, b, dims=NN):
    return lax.dot_general(a, b, dims, preferred_element_type=F32)


def flip(x, axis):
    return lax.ppermute(x, axis, ((0, 1), (1, 0)))


def pick(x, i, axis):
    return lax.dynamic_index_in_dim(x, i, axis, keepdims=False)


def ordered(mine, theirs, i, axis=0):
    return jnp.where(i == 0, jnp.stack([mine, theirs], axis), jnp.stack([theirs, mine], axis))


def gather_tokens(x, first, second):
    rows = x.shape[0]
    a = flip(x, first)
    b = flip(jnp.concatenate([x, a]), second)
    if first == "m":
        four = [x, a, b[:rows], b[rows:]]
    else:
        four = [x, b[:rows], a, b[rows:]]
    four = jnp.concatenate(four)
    return jnp.concatenate([four, flip(four, "core")])


def scatter_tokens(part):
    half = part.shape[0] // 2
    s = part[:half].astype(F32) + flip(part[half:], "core").astype(F32)
    half //= 2
    s = s[:half] + flip(s[half:].astype(BF), "replica").astype(F32)
    half //= 2
    return s[:half] + flip(s[half:].astype(BF), "m").astype(F32)


def line_gather(x, size, f):
    if size == 4:
        p1 = lax.ppermute(x, "f", ((0, 1), (1, 0), (2, 3), (3, 2)))
        p2 = lax.ppermute(x, "f", ((0, 2), (2, 0), (1, 3), (3, 1)))
        p3 = lax.ppermute(x, "f", ((1, 2), (2, 1)))
        p4 = lax.ppermute(p2, "f", ((2, 3), (1, 0)))
        p3 = jnp.where((f == 1) | (f == 2), p3, p4)
        lo, hi = f % 2, f // 2
        return ordered(
            ordered(x, p1, lo), ordered(p2, p3, lo), hi
        ).reshape((4,) + x.shape)
    blocks = [x]
    for k in range(1, size):
        blocks.append(lax.ppermute(x, "f", [(i, (i + k) % size) for i in range(size)]))
    order = (f - jnp.arange(size)) % size
    return jnp.take(jnp.stack(blocks), order, axis=0)


def line_scatter(parts, size, f):
    if size == 4:
        q = [pick(parts, f ^ r, 0) for r in range(4)]
        t = lax.ppermute(q[3], "f", ((0, 1), (3, 2)))
        q2 = jnp.where(
            (f == 1) | (f == 2), (q[2].astype(F32) + t.astype(F32)).astype(BF), q[2]
        )
        w = lax.ppermute(q[1], "f", ((0, 1), (1, 0), (2, 3), (3, 2)))
        v = lax.ppermute(q[3], "f", ((1, 2), (2, 1)))
        u = lax.ppermute(q2, "f", ((0, 2), (2, 0), (1, 3), (3, 1)))
        total = q[0].astype(F32) + w.astype(F32) + u.astype(F32)
        return jnp.where((f == 1) | (f == 2), total + v.astype(F32), total)
    total = pick(parts, f, 0).astype(F32)
    for k in range(1, size):
        sent = pick(parts, (f + k) % size, 0)
        total += lax.ppermute(sent, "f", [(i, (i + k) % size) for i in range(size)]).astype(F32)
    return total


def to_width(x, width):
    n = x.shape[1]
    x = jnp.pad(x, ((0, 0), (0, -n % width)))
    return jnp.concatenate([x[:, i : i + width] for i in range(0, x.shape[1], width)])


def from_width(p, rows, n):
    blocks = p.shape[0] // rows
    return jnp.concatenate([p[i * rows : (i + 1) * rows] for i in range(blocks)], axis=1)[:, :n]


def mlp_kernel(xh, cot, gain, shift, fc1, b1, fc2, normed, act, dup, sums):
    x = xh[...].astype(F32) * gain[...] + shift[...]
    x = x.astype(BF)
    normed[...] = x
    up = dot(x, fc1[...]) + b1[...]
    dact = dot(cot[...], fc2[...], NT)
    coeff = math.sqrt(2.0 / math.pi)
    square = up * up
    t = jnp.tanh(coeff * up * (1.0 + 0.044715 * square))
    half = 0.5 * (1.0 + t)
    act[...] = (up * half).astype(BF)
    slope = half + 0.5 * up * (1.0 - t * t) * coeff * (1.0 + 3.0 * 0.044715 * square)
    d = dact * slope
    dup[...] = d.astype(BF)

    @pl.when(pl.program_id(0) == 0)
    def _():
        sums[...] = jnp.zeros_like(sums)

    sums[...] += jnp.sum(d, axis=0, keepdims=True)


def att_kernel(
    heads, xn, xh, aux, cot, act, dup, wqkv, bqkv, wd, fc1, fc2, table,
    att, dqkv, out, dn, sums, lnsums,
):
    w = heads * HEAD_DIM
    qkv = dot(xn[...], wqkv[...]) + bqkv[...]
    datt = dot(cot[...], wd[...], NT).astype(BF)
    side = aux[...]
    trig = dot(side, table[...])
    cos, sin = trig[:, :w], trig[:, w:]
    lane = lax.broadcasted_iota(jnp.int32, (LEN, w), 1)
    low = lane % HEAD_DIM < ROTARY // 2

    def swap(v):
        return jnp.where(
            low, pltpu.roll(v, w - ROTARY // 2, axis=1), pltpu.roll(v, ROTARY // 2, axis=1)
        )

    q, k, v = qkv[:, :w], qkv[:, w : 2 * w], qkv[:, 2 * w :]
    q = (q * cos + swap(q) * sin).astype(BF)
    k = (k * cos + swap(k) * sin).astype(BF)
    v = v.astype(BF)
    seg = side[:, 97:98].astype(F32)
    one_hot = (lax.broadcasted_iota(jnp.int32, (8, 128), 1) == 97).astype(BF)
    seg_row = dot(one_hot, side, NT)[:1]
    rows = lax.broadcasted_iota(jnp.int32, (LEN, LEN), 0)
    cols = lax.broadcasted_iota(jnp.int32, (LEN, LEN), 1)
    allowed = (seg == seg_row) & (cols <= rows)
    scale = HEAD_DIM ** -0.5
    total_att = total_q = total_k = total_v = None
    for h in range(heads):
        mine = lane // HEAD_DIM == h
        zero = jnp.zeros_like(q)
        qh = jnp.where(mine, q, zero)
        dh = jnp.where(mine, datt, zero)
        s = dot(qh, k, NT) * scale
        s = jnp.where(allowed, s, -1e30)
        e = jnp.exp(s - jnp.max(s, axis=1, keepdims=True))
        p = e / jnp.sum(e, axis=1, keepdims=True)
        pb = p.astype(BF)
        dp = dot(dh, v, NT)
        delta = jnp.sum(p * dp, axis=1, keepdims=True)
        ds = (p * (dp - delta)).astype(BF)
        o = dot(pb, v)
        dq = dot(ds, k)
        dk = dot(ds, q, TN)
        dv = dot(pb, datt, TN)
        if h == 0:
            total_att, total_q, total_k, total_v = o, dq, dk, dv
        else:
            total_att = jnp.where(mine, o, total_att)
            total_q = jnp.where(mine, dq, total_q)
            total_k = jnp.where(mine, dk, total_k)
            total_v = jnp.where(mine, dv, total_v)
    ab = total_att.astype(BF)
    att[...] = ab
    dq = total_q * scale
    dk = total_k * scale
    dq = dq * cos - swap(dq) * sin
    dk = dk * cos - swap(dk) * sin
    d = jnp.concatenate([dq, dk, total_v], axis=1)
    db = d.astype(BF)
    dqkv[...] = db
    out[...] = (dot(act[...], fc2[...]) + dot(ab, wd[...])).astype(BF)
    g = dot(dup[...], fc1[...], NT) + dot(db, wqkv[...], NT)
    dn[...] = g.astype(BF)

    @pl.when(pl.program_id(0) == 0)
    def _():
        sums[...] = jnp.zeros_like(sums)
        lnsums[...] = jnp.zeros_like(lnsums)

    sums[...] += jnp.sum(d, axis=0, keepdims=True)
    lnsums[0:1, :] += jnp.sum(g * xh[...].astype(F32), axis=0, keepdims=True)
    lnsums[1:2, :] += jnp.sum(g, axis=0, keepdims=True)


def whole_block(shape):
    return pl.BlockSpec(shape, lambda i: (0,) * len(shape))


def row_block(width):
    return pl.BlockSpec((LEN, width), lambda i: (i, 0))


def call_mlp(xh, cot, gain, shift, fc1, b1, fc2):
    tokens = cot.shape[0]
    width, hidden = fc1.shape
    sds = jax.ShapeDtypeStruct
    return pl.pallas_call(
        mlp_kernel,
        grid=(tokens // LEN,),
        in_specs=[row_block(width), row_block(width)]
        + [whole_block(a.shape) for a in (gain, shift, fc1, b1, fc2)],
        out_specs=[row_block(width), row_block(hidden), row_block(hidden), whole_block((1, hidden))],
        out_shape=[
            sds((tokens, width), BF),
            sds((tokens, hidden), BF),
            sds((tokens, hidden), BF),
            sds((1, hidden), F32),
        ],
        cost_estimate=pl.CostEstimate(
            flops=4 * tokens * width * hidden, bytes_accessed=8 * tokens * width,
            transcendentals=tokens * hidden,
        ),
    )(xh, cot, gain, shift, fc1, b1, fc2)


def call_att(heads, xn, xh, cot, act, dup, wqkv, bqkv, wd, fc1, fc2, table):
    tokens, width = xn.shape
    hidden = act.shape[1]
    w = heads * HEAD_DIM
    sds = jax.ShapeDtypeStruct
    aux_at = width // 128
    return pl.pallas_call(
        functools.partial(att_kernel, heads),
        grid=(tokens // LEN,),
        in_specs=[
            row_block(width),
            row_block(width),
            pl.BlockSpec((LEN, 128), lambda i: (i, aux_at)),
            row_block(width),
            row_block(hidden),
            row_block(hidden),
        ]
        + [whole_block(a.shape) for a in (wqkv, bqkv, wd, fc1, fc2, table)],
        out_specs=[
            row_block(w),
            row_block(3 * w),
            row_block(width),
            row_block(width),
            whole_block((1, 3 * w)),
            whole_block((8, width)),
        ],
        out_shape=[
            sds((tokens, w), BF),
            sds((tokens, 3 * w), BF),
            sds((tokens, width), BF),
            sds((tokens, width), BF),
            sds((1, 3 * w), F32),
            sds((8, width), F32),
        ],
        cost_estimate=pl.CostEstimate(
            flops=4 * tokens * width * (hidden + 4 * w), bytes_accessed=12 * tokens * width,
            transcendentals=tokens * heads * LEN,
        ),
    )(xn, xh, xh, cot, act, dup, wqkv, bqkv, wd, fc1, fc2, table)


def side_columns(segment_ids, positions):
    half = ROTARY // 2
    freqs = 10000.0 ** (-(jnp.arange(half, dtype=F32) * 2.0 / ROTARY))
    angles = positions.astype(F32)[:, None] * freqs[None, :]

    def pieces(v):
        a = lax.reduce_precision(v, 8, 7)
        b = lax.reduce_precision(v - a, 8, 7)
        return [a, b, v - a - b]

    seg = segment_ids.reshape(-1, LEN)
    seg = (seg - seg[:, :1]).reshape(-1, 1).astype(F32)
    columns = pieces(jnp.cos(angles)) + pieces(jnp.sin(angles)) + [jnp.ones_like(seg), seg]
    columns = jnp.concatenate(columns, axis=1)
    return jnp.pad(columns, ((0, 0), (0, 128 - columns.shape[1]))).astype(BF)


def trig_table(heads):
    half = ROTARY // 2
    w = heads * HEAD_DIM
    table = np.zeros((128, 2 * w), np.float32)
    for lane in range(w):
        i = lane % HEAD_DIM
        if i >= ROTARY:
            table[96, lane] = 1.0
            continue
        for piece in range(3):
            table[piece * half + i % half, lane] = 1.0
            table[(3 + piece) * half + i % half, w + lane] = -1.0 if i < half else 1.0
    return jnp.asarray(table, BF)


def shards(
    size, hidden_in, segment_ids, positions, ln_gain, ln_bias, w_qkv, b_query, b_key, b_value,
    w_dense, b_dense, w_fc1, b_fc1, w_fc2, b_fc2, cotangent,
):
    y, f = lax.axis_index("replica"), lax.axis_index("f")
    m, c = lax.axis_index("m"), lax.axis_index("core")
    shard = (f * 2 + m) * 2 + c
    tokens, width = hidden_in.shape
    owners = 4 * size
    rows = w_qkv.shape[0]
    hidden = w_fc1.shape[1]
    piece = hidden // owners // 2
    all_heads = width // HEAD_DIM
    heads = all_heads // 8
    w = heads * HEAD_DIM
    by_block = rows == HEAD_DIM and size == 2 * heads

    cot = gather_tokens(cotangent.astype(BF), "m", "replica")
    center = hidden_in - jnp.mean(hidden_in, axis=-1, keepdims=True)
    variance = jnp.mean(center * center, axis=-1, keepdims=True)
    rstd = lax.rsqrt(variance + 1e-05)
    xhat = center * rstd
    xh = gather_tokens(
        jnp.concatenate([xhat.astype(BF), side_columns(segment_ids, positions)], axis=1),
        "replica", "m",
    )

    def eighths(a, y_axis):
        return pick(a, y, y_axis)

    fc1_of = w_fc1.reshape(rows, size, 2, 2, 2, piece)
    fc1_of = eighths(fc1_of, 4).transpose(2, 3, 0, 1, 4).reshape(2, 2, rows, size * piece)
    if by_block:
        qkv_of = w_qkv.reshape(rows, 3, 2, heads, 2, 2, HEAD_DIM)
        qkv_of = eighths(qkv_of, 2).transpose(3, 4, 0, 1, 2, 5)
    else:
        qkv_of = w_qkv.reshape(rows, 3, 2, 2, 2, heads, HEAD_DIM)
        qkv_of = eighths(qkv_of, 2).transpose(2, 3, 0, 1, 4, 5)
    qkv_of = qkv_of.reshape(2, 2, rows, 3 * w)

    vectors = (ln_gain, ln_bias, b_query, b_key, b_value, b_dense, b_fc1, b_fc2)
    cuts = np.cumsum([v.shape[0] for v in vectors])
    cw = size * piece
    small = jnp.concatenate(vectors)
    small_rows = -(-small.shape[0] // cw)
    small = jnp.pad(small, (0, small_rows * cw - small.shape[0])).reshape(small_rows, cw)

    def group_rows(a):
        own, other = pick(a, c, 1), pick(a, 1 - c, 1)
        both = ordered(own, flip(other, "core"), c)
        own, other = pick(both, m, 1), pick(both, 1 - m, 1)
        both = ordered(own, flip(other, "m"), m)
        return both.reshape(4 * rows, a.shape[-1])

    def with_small(a):
        more = jnp.broadcast_to(small, (2, 2) + small.shape)
        return jnp.concatenate([a, more], axis=2)

    own_fc1 = with_small(fc1_of)
    own, other = pick(own_fc1, c, 1), pick(own_fc1, 1 - c, 1)
    both = ordered(own, flip(other, "core"), c)
    own, other = pick(both, m, 1), pick(both, 1 - m, 1)
    both = ordered(own, flip(other, "m"), m)
    fc1_rows = both[:, :, :rows].reshape(4 * rows, cw)
    small_all = both[:, :, rows:].reshape(4 * small_rows, cw)
    own_fc2 = pick(w_fc2.reshape(2, piece, width), y, 0)
    pack = jnp.concatenate([fc1_rows, to_width(own_fc2, cw), small_all])
    pack = line_gather(pack, size, f)
    fc1 = pack[:, : 4 * rows].reshape(width, cw)
    blocks = -(-width // cw)
    fc2 = pack[:, 4 * rows : 4 * rows + blocks * piece].reshape(size, blocks, piece, cw)
    fc2 = fc2.transpose(0, 2, 1, 3).reshape(size * piece, blocks * cw)[:, :width]
    small_all = pack[:, 4 * rows + blocks * piece :].reshape(owners, small_rows * cw)
    gain, shift, bq, bk, bv, bd, b1, b2 = [
        small_all[:, a:b].astype(F32).reshape(-1) for a, b in zip([0, *cuts[:-1]], cuts)
    ]

    qkv_rows = group_rows(qkv_of)
    if by_block:
        pack = jnp.concatenate([qkv_rows, to_width(w_dense, 3 * w)])
        pack = line_gather(pack, size, f)
        wqkv = pack[:, : 4 * rows].reshape(width, 3 * w)
        half = size // 2
        wd = lax.dynamic_slice_in_dim(pack[:, 4 * rows :], y * half, half, 0)
        wd = wd.reshape(half, -1, rows, 3 * w).transpose(0, 2, 1, 3)
        wd = wd.reshape(w, -1)[:, :width]
    else:
        wqkv = line_gather(qkv_rows, size, f).reshape(width, 3 * w)
        wd = lax.all_gather(w_dense, ("f", "m", "core"), axis=0, tiled=True)
        wd = lax.dynamic_slice_in_dim(wd, ((y * 2 + m) * 2 + c) * w, w, 0)

    b1 = pick(pick(pick(b1.reshape(size, 2, 2, 2, piece), y, 3), c, 2), m, 1).reshape(1, cw)
    bk = jnp.pad(bk.reshape(all_heads, ROTARY), ((0, 0), (0, HEAD_DIM - ROTARY))).reshape(-1)
    bqkv = jnp.stack([bq, bk, bv])
    if by_block:
        bqkv = bqkv.reshape(3, 2, heads, 2, 2, HEAD_DIM)
        bqkv = pick(pick(pick(bqkv, c, 4), m, 3), y, 1)
    else:
        bqkv = bqkv.reshape(3, 2, 2, 2, heads, HEAD_DIM)
        bqkv = pick(pick(pick(bqkv, c, 3), m, 2), y, 1)
    bqkv = bqkv.reshape(1, 3 * w)

    normed, act, dup, sum_b1 = call_mlp(
        xh, cot, gain.reshape(1, -1), shift.reshape(1, -1), fc1, b1, fc2
    )
    grad_fc1 = dot(normed, dup, TN).astype(BF)
    grad_fc2 = dot(act, cot, TN).astype(BF)
    att, dqkv, out, dn, sum_qkv, sum_ln = call_att(
        heads, normed, xh, cot, act, dup, wqkv, bqkv, wd, fc1, fc2, trig_table(heads)
    )
    dn = scatter_tokens(dn)
    grad_qkv = dot(normed, dqkv, TN).astype(BF)
    grad_dense = dot(att, cot, TN).astype(BF)

    pack = jnp.concatenate(
        [
            grad_fc1.reshape(size, 4 * rows, cw),
            jax.vmap(lambda a: to_width(a, cw))(grad_fc2.reshape(size, piece, width)),
        ],
        axis=1,
    )
    pack = line_scatter(pack, size, f).astype(BF)
    fc1_part = pack[: 4 * rows].reshape(2, 2, rows, cw)
    fc2_part = from_width(pack[4 * rows :], piece, width)
    if by_block:
        half = size // 2
        dense_of = lax.dynamic_update_slice_in_dim(
            jnp.zeros((size, rows, width), BF), grad_dense.reshape(half, rows, width), y * half, 0
        )
        pack = jnp.concatenate(
            [
                grad_qkv.reshape(size, 4 * rows, 3 * w),
                jax.vmap(lambda a: to_width(a, 3 * w))(dense_of),
            ],
            axis=1,
        )
        pack = line_scatter(pack, size, f).astype(BF)
        qkv_part = pack[: 4 * rows].reshape(2, 2, rows, 3 * w)
        dense_part = from_width(pack[4 * rows :], rows, width)
    else:
        qkv_part = line_scatter(grad_qkv.reshape(size, 4 * rows, 3 * w), size, f).astype(BF)
        qkv_part = qkv_part.reshape(2, 2, rows, 3 * w)
        dense_of = lax.dynamic_update_slice_in_dim(
            jnp.zeros((width, width), BF), grad_dense, ((y * 2 + m) * 2 + c) * w, 0
        )
        dense_part = lax.psum_scatter(
            dense_of, ("f", "m", "core"), scatter_dimension=0, tiled=True
        )

    def eighths_of(g):
        both = ordered(pick(g, c, 1), flip(pick(g, 1 - c, 1), "core"), c)
        return ordered(pick(both, m, 1), flip(pick(both, 1 - m, 1), "m"), m)

    def both_replicas(g):
        return ordered(g, flip(g, "replica"), y)

    fc1_part = eighths_of(fc1_part).reshape(-1, cw)
    n1 = fc1_part.shape[0]
    pack = both_replicas(jnp.concatenate([fc1_part, to_width(fc2_part, cw)]))
    g = pack[:, :n1].reshape(2, 2, 2, rows, size, piece)
    grad_w_fc1 = g.transpose(3, 4, 1, 2, 0, 5).reshape(rows, hidden).astype(F32)
    grad_w_fc2 = jnp.concatenate(
        [from_width(pack[i, n1:], piece, width) for i in range(2)]
    ).astype(F32)
    qkv_part = eighths_of(qkv_part).reshape(-1, 3 * w)
    n1 = qkv_part.shape[0]
    pack = both_replicas(jnp.concatenate([qkv_part, to_width(dense_part, 3 * w)]))
    g = pack[:, :n1].reshape(2, 2, 2, rows, 3, heads, HEAD_DIM)
    if by_block:
        g = g.transpose(3, 4, 0, 5, 1, 2, 6)
    else:
        g = g.transpose(3, 4, 0, 1, 2, 5, 6)
    grad_w_qkv = g.reshape(rows, 3 * width).astype(F32)
    g = pack[:, n1:].astype(F32)
    grad_w_dense = from_width(g[0] + g[1], rows, width)

    zero = jnp.zeros((2, 2, 2, cw), F32)
    at = (y, m, c)
    sum_b1 = lax.dynamic_update_slice(zero, sum_b1.reshape(1, 1, 1, cw), at + (0,))
    sum_b1 = sum_b1.reshape(2, 2, 2, size, piece).transpose(3, 1, 2, 0, 4).reshape(-1)
    zero = jnp.zeros((2, 2, 2, 3 * w), F32)
    sum_qkv = lax.dynamic_update_slice(zero, sum_qkv.reshape(1, 1, 1, 3 * w), at + (0,))
    sum_qkv = sum_qkv.reshape(2, 2, 2, 3, heads, HEAD_DIM)
    if by_block:
        sum_qkv = sum_qkv.transpose(3, 0, 4, 1, 2, 5).reshape(-1)
    else:
        sum_qkv = sum_qkv.transpose(3, 0, 1, 2, 4, 5).reshape(-1)
    vec = jnp.concatenate(
        [sum_b1, sum_qkv, sum_ln[0], sum_ln[1], jnp.sum(cotangent, axis=0)]
    ).reshape(-1, 128)
    for axis in ("core", "m", "replica"):
        vec = vec + flip(vec, axis)
    vec = jnp.sum(line_gather(vec, size, f), axis=0).reshape(-1)

    def own(a, count):
        return lax.dynamic_slice_in_dim(vec, a + shard * count, count)

    grad_b_fc1 = own(0, hidden // owners)
    a = hidden
    grad_b_query = own(a, rows)
    key_sums = vec[a + width : a + 2 * width].reshape(all_heads, HEAD_DIM)[:, :ROTARY].reshape(-1)
    grad_b_key = lax.dynamic_slice_in_dim(
        key_sums, shard * (key_sums.shape[0] // owners), key_sums.shape[0] // owners
    )
    grad_b_value = own(a + 2 * width, rows)
    a += 3 * width
    grad_ln_gain = own(a, rows)
    grad_ln_bias = own(a + width, rows)
    grad_b_out = own(a + 2 * width, rows)

    block_out = hidden_in + scatter_tokens(out) + (bd + b2)[None, :]
    g = dn * gain[None, :]
    grad_input = cotangent + rstd * (
        g
        - jnp.mean(g, axis=-1, keepdims=True)
        - xhat * jnp.mean(g * xhat, axis=-1, keepdims=True)
    )
    return (
        block_out, grad_input, grad_ln_gain, grad_ln_bias, grad_w_qkv, grad_b_query, grad_b_key,
        grad_b_value, grad_w_dense, grad_b_out, grad_w_fc1, grad_b_fc1, grad_w_fc2, grad_b_out,
    )


def solution(mesh):
    replicas, owners = mesh.devices.shape
    size = owners // 4
    grid = Mesh(mesh.devices.reshape(replicas, size, 2, 2), ("replica", "f", "m", "core"))
    everything = P(("replica", "f", "m", "core"))
    owner = P(("f", "m", "core"))
    return jax.shard_map(
        functools.partial(shards, size),
        mesh=grid,
        in_specs=(everything,) * 3 + (owner,) * 12 + (everything,),
        out_specs=(everything,) * 2 + (owner,) * 12,
        check_vma=False,
    )
```
